256 devices in a mesh: row: 8 (over x, core), col: 32 (over y, z).
Axes of the slice: x: 4, y: 4, z: 8, core: 2. Of those that a mesh axis runs over, the one named last changes fastest.
Arguments:
- trailing: float32 [4096, 16384], P('row', 'col'), may hold values from -6 to 6
- panel_factors: float32 [4096, 256], P('row', 'col'), as said below
- pivots: int32 [256], replicated, may hold values from 0 to 4095, as said below
Outputs:
- applied: float32 [4096, 16384], P('row', 'col')
The draws below stay inside these ranges and needn't reach their ends.
Inputs may be any that keep to these rules, and one draw needn't show every extreme that they name: pivots[j] lies between j and 4095. `panel_factors`: the strictly lower part of the first 256 rows keeps unit_lower well conditioned.
All inputs are finite; a program needn't handle non-finite values.
Results may differ from the reference program's by a relative error of at most 0.000059.
Values sent between devices are 32-bit elements; how exact they have to be, the bound alone decides.
No kernel may reach another device: no remote copies, remote signals or barrier semaphores. Data moves between devices by JAX's collectives and lax.ppermute only.
A program may use at most 64 MiB of HBM per device.

```python
import jax
import jax.numpy as jnp
from jax import lax

NB = 256
ROWS = 4096
NC = 16384


def draw_panel_factors(key, part):
    base = jax.random.normal(key, (ROWS, NB), jnp.float32)
    top_block = base[:NB] * (0.5 / NB ** 0.5)
    below = base[NB:] * (1.0 / NB ** 0.5)
    return jnp.concatenate([top_block, below], axis=0)


def draw_pivots(key, part):
    raw_bits = jax.random.randint(jax.random.fold_in(key, 7), (NB,), 0, 1073741824, dtype=jnp.int32)
    column = jnp.arange(NB, dtype=jnp.int32)
    return column + raw_bits % (ROWS - column)


def block_levels(own_key, dims, split, low, largest):
    def one(dim, shards_of):
        steps = jax.random.uniform(jax.random.fold_in(jax.random.fold_in(own_key, 6), dim), (shards_of,), jnp.float32, low / len(split), largest / len(split))
        return jnp.repeat(jnp.exp(steps), dims[dim] // shards_of).reshape((-1,) + (1,) * (len(dims) - dim - 1))

    gain = one(*split[0])
    for cut in split[1:]:
        gain = gain * one(*cut)
    return gain


def normal_values(rng, shape, width, bound, shards=(), kind=jnp.bfloat16):
    array = width * jax.random.normal(rng, shape, jnp.float32)
    if shards:
        array = array * block_levels(rng, shape, shards, -0.22, 0.18)
    return jnp.clip(array, -bound, bound).astype(kind)


def setup_inputs(seed: int = 0) -> dict:
    keys = jax.random.split(jax.random.key(seed), 4)
    trailing = normal_values(keys[0], (ROWS, NC), 1.0, 6.0, ((0, 8), (1, 32)), jnp.float32)
    panel_factors = draw_panel_factors(jax.random.fold_in(keys[3], 71), 0)
    pivots = draw_pivots(jax.random.fold_in(keys[3], 71), 0)
    return dict(trailing=trailing, panel_factors=panel_factors, pivots=pivots)


def reference(trailing, panel_factors, pivots):

    def swap_step(column, row_order):
        target = pivots[column]
        first_val = row_order[column]
        second_val = row_order[target]
        return row_order.at[column].set(second_val).at[target].set(first_val)
    row_order = lax.fori_loop(0, NB, swap_step, jnp.arange(ROWS, dtype=jnp.int32))
    swapped = jnp.take(trailing, row_order, axis=0)
    unit_lower = jnp.tril(panel_factors[:NB], -1) + jnp.eye(NB, dtype=jnp.float32)
    upper_rows = jax.scipy.linalg.solve_triangular(unit_lower, swapped[:NB], lower=True, unit_diagonal=True)
    lower_part = swapped[NB:] - jnp.dot(panel_factors[NB:].astype(jnp.float32), upper_rows.astype(jnp.float32), precision=lax.Precision.HIGHEST, preferred_element_type=jnp.float32)
    return jnp.concatenate([upper_rows, lower_part], axis=0)
```

```python
import jax
import jax.numpy as jnp
from jax import lax
from jax.experimental import pallas as pl
from jax.experimental.pallas import tpu as pltpu
from jax.sharding import Mesh
from jax.sharding import PartitionSpec as P

ROW = ("x", "core")
COL = ("y", "z")
HIGHEST = lax.Precision.HIGHEST
VMEM = pl.BlockSpec(memory_space=pltpu.VMEM)
SMEM = pl.BlockSpec(memory_space=pltpu.SMEM)


def f32(*shape):
    return jax.ShapeDtypeStruct(shape, jnp.float32)


def chip_shift(value, step):
    return lax.ppermute(value, "x", [(i, (i + step) % 4) for i in range(4)])


def core_swap(value):
    return lax.ppermute(value, "core", [(0, 1), (1, 0)])


def plan_kernel(piv, where_am_i, t_ref, keep, send, meta, source, displaced, order):
    width = piv.shape[0]
    half = width // 2
    rows = t_ref.shape[0]
    chip, core = where_am_i[0], where_am_i[1]
    device = chip * 2 + core
    first = device * rows

    def init(j, carry):
        p = piv[j]
        order[p] = p
        order[j] = j
        return carry

    lax.fori_loop(0, width, init, 0, unroll=8)

    def swap(j, carry):
        p = piv[j]
        a = order[j]
        b = order[p]
        order[j] = b
        order[p] = a
        return carry

    lax.fori_loop(0, width, swap, 0, unroll=8)

    def gather(i, out, slot):
        src = order[slot]
        down = order[src]
        source[slot] = src
        displaced[slot] = down
        meta[pl.ds(slot, 1), :] = jnp.full((1, 128), src, jnp.int32)
        own = (src >= first) & (src < first + rows)
        row = jnp.where(own, src - first, jnp.where(device == 0, down, 0))
        out[pl.ds(i, 1), :] = t_ref[pl.ds(row, 1), :]

    def both(i, carry):
        gather(i, send, (1 - core) * half + i)
        gather(i, keep, core * half + i)
        return carry

    lax.fori_loop(0, half, both, 0, unroll=4)


def owner_of(meta_rows, rows):
    device = meta_rows // rows
    device = jnp.concatenate([device] * 4, axis=1)
    return device // 2, device % 2


def combine_kernel(where_am_i, keep, got, meta, joined, p1, p2, p3):
    chip, core = where_am_i[0], where_am_i[1]
    half = keep.shape[0]
    part = half // 4
    owner_chip, owner_core = owner_of(meta[pl.ds(core * half, half), :], keep.shape[1])
    mine = owner_chip == chip
    other = (mine & (owner_core != core)) | (~mine & ((chip == 0) & (core == 1)))
    joined[...] = jnp.where(other, got[...], keep[...])
    for step, out in ((1, p1), (2, p2), (3, p3)):
        out[...] = joined[pl.ds(lax.rem(chip + step, 4) * part, part), :]


def route_kernel(where_am_i, joined, r1, r2, r3, meta, m0, m1, m2, m3):
    chip, core = where_am_i[0], where_am_i[1]
    half = joined.shape[0]
    part = half // 4
    owner_chip, _ = owner_of(
        meta[pl.ds(core * half + chip * part, part), :], joined.shape[1]
    )
    own = joined[pl.ds(chip * part, part), :]
    a, b, c = r1[...], r2[...], r3[...]
    behind = lax.rem(chip - owner_chip + 4, 4)
    pivot_row = jnp.where(
        behind == 0, own, jnp.where(behind == 1, a, jnp.where(behind == 2, b, c))
    )
    top_row = jnp.where(
        chip == 0, own, jnp.where(chip == 1, a, jnp.where(chip == 2, b, c))
    )
    for step, out in enumerate((m0, m1, m2, m3)):
        out[...] = jnp.where(
            owner_chip == lax.rem(chip + step, 4), top_row, pivot_row
        )


def halves_kernel(
    where_am_i, n0, n1, n2, n3, joined, keep, got, meta, message, pivot_half, top_half, g
):
    chip, core = where_am_i[0], where_am_i[1]
    half = joined.shape[0]
    part = half // 4
    for step, src in enumerate((n0, n1, n2, n3)):
        g[pl.ds(lax.rem(chip - step + 4, 4) * part, part), :] = src[...]
    owner_chip, owner_core = owner_of(meta[pl.ds(core * half, half), :], joined.shape[1])
    mine = owner_chip == chip
    routed = g[...]
    rows = joined[...]
    pivot_half[...] = jnp.where(mine, rows, routed)
    first_device = (chip == 0) & (core == 0)
    message[...] = jnp.where(
        mine & first_device,
        keep[...],
        jnp.where(mine & (owner_core == core), rows, routed),
    )
    top_half[...] = jnp.where(chip == 0, got[...], routed)


def final_kernel(
    where_am_i, source, displaced, t_ref, w_ref, pivot_half, top_half, send, got, meta, out, pivot
):
    chip, core = where_am_i[0], where_am_i[1]
    rows = t_ref.shape[0]
    half = pivot_half.shape[0]
    width = 2 * half
    device = chip * 2 + core
    first = device * rows
    out[...] = t_ref[...]

    def place(i, slot, tops):
        src = source[slot]

        @pl.when((src >= first) & (src < first + rows) & (src >= width))
        def _():
            @pl.when(device == 0)
            def _():
                out[pl.ds(src - first, 1), :] = t_ref[pl.ds(displaced[slot], 1), :]

            @pl.when(device != 0)
            def _():
                out[pl.ds(src - first, 1), :] = tops[pl.ds(i, 1), :]

    def both(i, carry):
        place(i, core * half + i, top_half)
        place(i, (1 - core) * half + i, got)
        return carry

    lax.fori_loop(0, half, both, 0, unroll=2)

    @pl.when(device == 0)
    def _():
        out[0:width, :] = jnp.zeros((width, out.shape[1]), jnp.float32)

    owner_chip, owner_core = owner_of(meta[pl.ds((1 - core) * half, half), :], rows)
    here = (owner_chip == chip) & (owner_core == core)
    pivot[pl.ds(core * half, half), :] = pivot_half[...]
    pivot[pl.ds((1 - core) * half, half), :] = jnp.where(here, send[...], got[...])
    out[...] -= jnp.dot(
        w_ref[...], pivot[...], precision=HIGHEST, preferred_element_type=jnp.float32
    )


def weights_kernel(where_am_i, stacked, w_ref):
    width = stacked.shape[0]
    rows = stacked.shape[1] - width
    square = stacked[:, rows:]
    row = lax.broadcasted_iota(jnp.int32, (width, width), 0)
    col = lax.broadcasted_iota(jnp.int32, (width, width), 1)
    inv = jnp.where(row == col, 1.0, 0.0)
    size = 1
    while size < width:
        link = (
            (row // (2 * size) == col // (2 * size))
            & (row // size % 2 == 0)
            & (col // size % 2 == 1)
        )
        off = jnp.where(link, square, 0.0)
        if size == 1:
            inv = inv - off
        else:
            left = jnp.dot(inv, off, precision=HIGHEST, preferred_element_type=jnp.float32)
            inv = inv - jnp.dot(
                left, inv, precision=HIGHEST, preferred_element_type=jnp.float32
            )
        size *= 2
    weights = jnp.dot(
        inv, stacked[:, :rows], precision=HIGHEST, preferred_element_type=jnp.float32
    )
    w_ref[...] = weights.T

    @pl.when((where_am_i[0] == 0) & (where_am_i[1] == 0))
    def _():
        w_ref[0:width, :] = -inv.T


def on_device(trailing, panel_factors, pivots):
    rows, columns = trailing.shape
    width = pivots.shape[0]
    half, part = width // 2, width // 8
    chip, core = lax.axis_index("x"), lax.axis_index("core")
    here = jnp.stack([chip, core]).astype(jnp.int32)

    panel = panel_factors.T
    square = panel[:, :width]
    square = jnp.where(core == 1, lax.ppermute(square, "core", [(0, 1)]), square)
    square = jnp.where(chip == 2, lax.ppermute(square, "x", [(0, 2)]), square)
    square = jnp.where(
        chip % 2 == 1, lax.ppermute(square, "x", [(0, 1), (2, 3)]), square
    )
    block = jnp.concatenate([panel, square], axis=1)
    copies = jnp.broadcast_to(block, (lax.axis_size(COL), *block.shape))
    stacked = lax.all_to_all(copies, COL, split_axis=0, concat_axis=0, tiled=True)
    stacked = stacked.reshape(width, rows + width)
    weights = pl.pallas_call(
        weights_kernel,
        out_shape=f32(rows, width),
        in_specs=[SMEM, VMEM],
        out_specs=VMEM,
    )(here, stacked)

    index = jax.ShapeDtypeStruct((width,), jnp.int32)
    keep, send, meta, source, displaced = pl.pallas_call(
        plan_kernel,
        out_shape=(
            f32(half, columns),
            f32(half, columns),
            jax.ShapeDtypeStruct((width, 128), jnp.int32),
            index,
            index,
        ),
        in_specs=[SMEM, SMEM, VMEM],
        out_specs=(VMEM, VMEM, VMEM, SMEM, SMEM),
        scratch_shapes=[pltpu.SMEM((rows * 8,), jnp.int32)],
    )(pivots, here, trailing)
    got = core_swap(send)
    joined, p1, p2, p3 = pl.pallas_call(
        combine_kernel,
        out_shape=(f32(half, columns),) + (f32(part, columns),) * 3,
        in_specs=[SMEM, VMEM, VMEM, VMEM],
        out_specs=(VMEM,) * 4,
    )(here, keep, got, meta)
    r1, r2, r3 = (chip_shift(p, s) for s, p in ((1, p1), (2, p2), (3, p3)))
    m0, m1, m2, m3 = pl.pallas_call(
        route_kernel,
        out_shape=(f32(part, columns),) * 4,
        in_specs=[SMEM] + [VMEM] * 5,
        out_specs=(VMEM,) * 4,
    )(here, joined, r1, r2, r3, meta)
    n1, n2, n3 = (chip_shift(m, s) for s, m in ((1, m1), (2, m2), (3, m3)))
    message, pivot_half, top_half = pl.pallas_call(
        halves_kernel,
        out_shape=(f32(half, columns),) * 3,
        in_specs=[SMEM] + [VMEM] * 8,
        out_specs=(VMEM,) * 3,
        scratch_shapes=[pltpu.VMEM((half, columns), jnp.float32)],
    )(here, m0, n1, n2, n3, joined, keep, got, meta)
    last = core_swap(message)
    return pl.pallas_call(
        final_kernel,
        out_shape=f32(rows, columns),
        in_specs=[SMEM, SMEM, SMEM] + [VMEM] * 7,
        out_specs=VMEM,
        scratch_shapes=[pltpu.VMEM((width, columns), jnp.float32)],
    )(here, source, displaced, trailing, weights, pivot_half, top_half, send, last, meta)


def solution(mesh):
    torus = Mesh(mesh.devices.reshape(4, 2, 4, 8), ("x", "core", "y", "z"))
    return jax.shard_map(
        on_device,
        mesh=torus,
        in_specs=(P(ROW, COL), P(ROW, COL), P()),
        out_specs=P(ROW, COL),
        check_vma=False,
    )
```

```python
import jax
import jax.numpy as jnp
from jax import lax
from jax.experimental import pallas as pl
from jax.experimental.pallas import tpu as pltpu
from jax.sharding import Mesh
from jax.sharding import PartitionSpec as P

ROW = ("x", "core")
COL = ("y", "z")
PARAMS = pltpu.CompilerParams(vmem_limit_bytes=12 * 1024 * 1024)
VMEM = pl.BlockSpec(memory_space=pltpu.VMEM)
SMEM = pl.BlockSpec(memory_space=pltpu.SMEM)


def f32(*shape):
    return jax.ShapeDtypeStruct(shape, jnp.float32)


def chip_shift(value, step):
    return lax.ppermute(value, "x", [(i, (i + step) % 4) for i in range(4)])


def split(value):
    high = value.astype(jnp.bfloat16)
    return high, (value - high.astype(jnp.float32)).astype(jnp.bfloat16)


def product(left, right):
    def dot(a, b):
        return jnp.dot(a, b, preferred_element_type=jnp.float32)

    return dot(left[0], right[0]) + (dot(left[0], right[1]) + dot(left[1], right[0]))


def core_swap(value):
    return lax.ppermute(value, "core", [(0, 1), (1, 0)])


def plan_kernel(piv, where_am_i, t_ref, keep, send, meta, places, order, picks):
    width = piv.shape[0]
    half = width // 2
    rows = t_ref.shape[0]
    shift = rows.bit_length() - 1
    chip, core = where_am_i[0], where_am_i[1]
    device = chip * 2 + core
    first = device * rows

    def init(j, carry):
        p = piv[j]
        order[p] = p
        order[j] = j
        return carry

    lax.fori_loop(0, width, init, 0, unroll=16)

    def swap(j, carry):
        p = piv[j]
        a = order[j]
        b = order[p]
        order[j] = b
        order[p] = a
        return carry

    lax.fori_loop(0, width, swap, 0, unroll=16)

    def pick(slot, count):
        src = order[slot]
        down = order[src]
        local = src - first
        own = (local >= 0) & (local < rows)
        picks[slot] = jnp.where(own, local, jnp.where(device == 0, down, 0))
        picks[width + slot] = lax.shift_right_logical(src, shift)
        places[1 + count] = slot
        places[1 + width + count] = local
        places[1 + 2 * width + count] = down
        return count + jnp.where(own & (src >= width), 1, 0)

    places[0] = lax.fori_loop(0, width, pick, 0, unroll=8)

    def gather(i, carry):
        for base, out in ((core * half, keep), ((1 - core) * half, send)):
            slot = base + i
            out[pl.ds(i, 1), :] = t_ref[pl.ds(picks[slot], 1), :]
            meta[pl.ds(slot, 1), :] = jnp.full((1, 128), picks[width + slot], jnp.int32)
        return carry

    lax.fori_loop(0, half, gather, 0, unroll=8)


def owner_of(device, columns):
    device = jnp.concatenate([device] * (columns // 128), axis=1)
    return lax.shift_right_logical(device, 1), device & 1


def combine_kernel(where_am_i, keep, got, meta, joined, p1, p2, p3):
    chip, core = where_am_i[0], where_am_i[1]
    half = keep.shape[0]
    part = half // 4
    owner_chip, owner_core = owner_of(meta[pl.ds(core * half, half), :], keep.shape[1])
    mine = owner_chip == chip
    other = (mine & (owner_core != core)) | (~mine & ((chip == 0) & (core == 1)))
    joined[...] = jnp.where(other, got[...], keep[...])
    for step, out in ((1, p1), (2, p2), (3, p3)):
        out[...] = joined[pl.ds(lax.rem(chip + step, 4) * part, part), :]


def route_kernel(where_am_i, joined, r1, r2, r3, meta, m0, m1, m2, m3):
    chip, core = where_am_i[0], where_am_i[1]
    half = joined.shape[0]
    part = half // 4
    owner_chip, _ = owner_of(
        meta[pl.ds(core * half + chip * part, part), :], joined.shape[1]
    )
    own = joined[pl.ds(chip * part, part), :]
    a, b, c = r1[...], r2[...], r3[...]
    behind = (chip - owner_chip) & 3
    pivot_row = jnp.where(
        behind == 0, own, jnp.where(behind == 1, a, jnp.where(behind == 2, b, c))
    )
    top_row = jnp.where(
        chip == 0, own, jnp.where(chip == 1, a, jnp.where(chip == 2, b, c))
    )
    for step, out in enumerate((m0, m1, m2, m3)):
        out[...] = jnp.where(
            owner_chip == lax.rem(chip + step, 4), top_row, pivot_row
        )


def halves_kernel(
    where_am_i, n0, n1, n2, n3, joined, keep, got, meta, message, pivot_half, top_half, g
):
    chip, core = where_am_i[0], where_am_i[1]
    half = joined.shape[0]
    part = half // 4
    for step, src in enumerate((n0, n1, n2, n3)):
        g[pl.ds(lax.rem(chip - step + 4, 4) * part, part), :] = src[...]
    owner_chip, owner_core = owner_of(meta[pl.ds(core * half, half), :], joined.shape[1])
    mine = owner_chip == chip
    routed = g[...]
    rows = joined[...]
    pivot_half[...] = jnp.where(mine, rows, routed)
    first_device = (chip == 0) & (core == 0)
    message[...] = jnp.where(
        mine & first_device,
        keep[...],
        jnp.where(mine & (owner_core == core), rows, routed),
    )
    top_half[...] = jnp.where(chip == 0, got[...], routed)


def final_kernel(
    where_am_i, places, t_ref, wh_ref, wl_ref, pivot_half, top_half, send, got, meta, out, pivot
):
    chip, core = where_am_i[0], where_am_i[1]
    rows = t_ref.shape[0]
    half = pivot_half.shape[0]
    width = 2 * half
    device = chip * 2 + core
    owner_chip, owner_core = owner_of(
        meta[pl.ds((1 - core) * half, half), :], got.shape[1]
    )
    here = (owner_chip == chip) & (owner_core == core)
    pivot[pl.ds(core * half, half), :] = pivot_half[...]
    pivot[pl.ds((1 - core) * half, half), :] = jnp.where(here, send[...], got[...])
    out[...] = t_ref[...]

    def place(i, carry):
        slot = places[1 + i]
        target = pl.ds(places[1 + width + i], 1)
        in_half = (slot >= half) == (core == 1)
        index = slot & (half - 1)
        late = jnp.where(in_half, 1, 0)
        row = jnp.where(
            device == 0,
            t_ref[pl.ds(jnp.where(device == 0, places[1 + 2 * width + i], 0), 1), :],
            jnp.where(
                late == 1, top_half[pl.ds(index, 1), :], got[pl.ds(index, 1), :]
            ),
        )
        out[target, :] = row
        return carry

    lax.fori_loop(0, places[0], place, 0)

    @pl.when(device == 0)
    def _():
        out[0:width, :] = jnp.zeros((width, out.shape[1]), jnp.float32)

    weights = wh_ref[...], wl_ref[...]
    out[...] -= product(weights, split(pivot[...]))


def weights_kernel(where_am_i, stacked, wh_ref, wl_ref):
    width = stacked.shape[0]
    rows = stacked.shape[1] - width
    square = stacked[:, rows:]
    row = lax.broadcasted_iota(jnp.int32, (width, width), 0)
    col = lax.broadcasted_iota(jnp.int32, (width, width), 1)
    apart = row ^ col
    inv = jnp.where(row == col, 1.0, 0.0)
    level = 0
    while (1 << level) < width:
        size = 1 << level
        link = (lax.shift_right_logical(apart, level) == 1) & ((col & size) != 0)
        off = jnp.where(link, square, 0.0)
        if level == 0:
            inv = inv - off
        else:
            parts = split(inv)
            inv = inv - product(split(product(parts, split(off))), parts)
        level += 1
    weights = product(split(inv), split(stacked[:, :rows])).T
    high, low = split(weights)
    wh_ref[...] = high
    wl_ref[...] = low

    @pl.when((where_am_i[0] == 0) & (where_am_i[1] == 0))
    def _():
        high, low = split(-inv.T)
        wh_ref[0:width, :] = high
        wl_ref[0:width, :] = low


def on_device(trailing, panel_factors, pivots):
    rows, columns = trailing.shape
    width = pivots.shape[0]
    half, part = width // 2, width // 8
    chip, core = lax.axis_index("x"), lax.axis_index("core")
    here = jnp.stack([chip, core]).astype(jnp.int32)

    panel = panel_factors.T
    square = panel[:, :width]
    square = jnp.where(core == 1, lax.ppermute(square, "core", [(0, 1)]), square)
    square = jnp.where(chip == 2, lax.ppermute(square, "x", [(0, 2)]), square)
    square = jnp.where(
        chip % 2 == 1, lax.ppermute(square, "x", [(0, 1), (2, 3)]), square
    )
    block = jnp.concatenate([panel, square], axis=1)
    copies = jnp.broadcast_to(block, (lax.axis_size(COL), *block.shape))
    stacked = lax.all_to_all(copies, COL, split_axis=0, concat_axis=0, tiled=True)
    stacked = stacked.reshape(width, rows + width)
    half_weights = jax.ShapeDtypeStruct((rows, width), jnp.bfloat16)
    high, low = pl.pallas_call(
        weights_kernel,
        out_shape=(half_weights, half_weights),
        in_specs=[SMEM, VMEM],
        out_specs=(VMEM, VMEM),
        compiler_params=PARAMS,
    )(here, stacked)

    keep, send, meta, places = pl.pallas_call(
        plan_kernel,
        out_shape=(
            f32(half, columns),
            f32(half, columns),
            jax.ShapeDtypeStruct((width, 128), jnp.int32),
            jax.ShapeDtypeStruct((1024,), jnp.int32),
        ),
        in_specs=[SMEM, SMEM, VMEM],
        out_specs=(VMEM, VMEM, VMEM, SMEM),
        scratch_shapes=[
            pltpu.SMEM((rows * 8,), jnp.int32),
            pltpu.SMEM((2 * width,), jnp.int32),
        ],
        compiler_params=PARAMS,
    )(pivots, here, trailing)
    got = core_swap(send)
    joined, p1, p2, p3 = pl.pallas_call(
        combine_kernel,
        out_shape=(f32(half, columns),) + (f32(part, columns),) * 3,
        in_specs=[SMEM, VMEM, VMEM, VMEM],
        out_specs=(VMEM,) * 4,
        compiler_params=PARAMS,
    )(here, keep, got, meta)
    r1, r2, r3 = (chip_shift(p, s) for s, p in ((1, p1), (2, p2), (3, p3)))
    m0, m1, m2, m3 = pl.pallas_call(
        route_kernel,
        out_shape=(f32(part, columns),) * 4,
        in_specs=[SMEM] + [VMEM] * 5,
        out_specs=(VMEM,) * 4,
        compiler_params=PARAMS,
    )(here, joined, r1, r2, r3, meta)
    n1, n2, n3 = (chip_shift(m, s) for s, m in ((1, m1), (2, m2), (3, m3)))
    message, pivot_half, top_half = pl.pallas_call(
        halves_kernel,
        out_shape=(f32(half, columns),) * 3,
        in_specs=[SMEM] + [VMEM] * 8,
        out_specs=(VMEM,) * 3,
        scratch_shapes=[pltpu.VMEM((half, columns), jnp.float32)],
        compiler_params=PARAMS,
    )(here, m0, n1, n2, n3, joined, keep, got, meta)
    last = core_swap(message)
    return pl.pallas_call(
        final_kernel,
        out_shape=f32(rows, columns),
        in_specs=[SMEM, SMEM] + [VMEM] * 8,
        out_specs=VMEM,
        scratch_shapes=[pltpu.VMEM((width, columns), jnp.float32)],
        compiler_params=PARAMS,
    )(here, places, trailing, high, low, pivot_half, top_half, send, last, meta)


def solution(mesh):
    torus = Mesh(mesh.devices.reshape(4, 2, 4, 8), ("x", "core", "y", "z"))
    return jax.shard_map(
        on_device,
        mesh=torus,
        in_specs=(P(ROW, COL), P(ROW, COL), P()),
        out_specs=P(ROW, COL),
        check_vma=False,
    )
```

```python
import jax
import jax.numpy as jnp
from jax import lax
from jax.experimental import pallas as pl
from jax.experimental.pallas import tpu as pltpu
from jax.sharding import Mesh
from jax.sharding import PartitionSpec as P


ROW = ("x", "core")
COL = ("y", "z")
PARAMS = pltpu.CompilerParams(vmem_limit_bytes=12 * 1024 * 1024)
VMEM = pl.BlockSpec(memory_space=pltpu.VMEM)
SMEM = pl.BlockSpec(memory_space=pltpu.SMEM)


def f32(*shape):
    return jax.ShapeDtypeStruct(shape, jnp.float32)


def along(value, axis, step):
    size = lax.axis_size(axis)
    return lax.ppermute(value, axis, [(i, (i + step) % size) for i in range(size)])


def swapped(value, axis, bit):
    return lax.ppermute(value, axis, [(i, i ^ bit) for i in range(lax.axis_size(axis))])


def split(value):
    high = value.astype(jnp.bfloat16)
    return high, (value - high.astype(jnp.float32)).astype(jnp.bfloat16)


def product(left, right):
    def dot(a, b):
        return jnp.dot(a, b, preferred_element_type=jnp.float32)

    return dot(left[0], right[0]) + (dot(left[0], right[1]) + dot(left[1], right[0]))


def plan_kernel(piv, where_am_i, t_hbm, keep, send, meta, places, order, picks, t_ref, arrived):
    fetch = pltpu.make_async_copy(t_hbm, t_ref, arrived)
    fetch.start()
    width = piv.shape[0]
    half = width // 2
    rows = t_ref.shape[0]
    shift = rows.bit_length() - 1
    chip, core = where_am_i[0], where_am_i[1]
    device = chip * 2 + core

    def init(j, carry):
        p = piv[j]
        order[p] = p
        order[j] = j
        return carry

    lax.fori_loop(0, width, init, 0, unroll=16)

    def swap(j, carry):
        p = piv[j]
        a = order[j]
        b = order[p]
        order[j] = b
        order[p] = a
        return carry

    lax.fori_loop(0, width, swap, 0, unroll=16)

    def pick(slot, count):
        src = order[slot]
        down = order[src]
        local = src & (rows - 1)
        own = lax.shift_right_logical(src, shift) == device
        picks[slot] = jnp.where(own, local, down & (rows - 1))
        places[1 + count] = slot | (local << 8) | (down << 20)
        return count + jnp.where(own & (src >= width), 1, 0)

    places[0] = lax.fori_loop(0, width, pick, 0, unroll=8)

    def gather(group, carry):
        for base, out in ((core * half, keep), ((1 - core) * half, send)):
            for k in range(8):
                start = pl.multiple_of(group * 8, 8)
                slot = base + start + k
                out[pl.ds(start + k, 1), :] = t_ref[pl.ds(picks[slot], 1), :]
                owner = lax.shift_right_logical(order[slot], shift)
                meta[pl.ds(pl.multiple_of(base, half) + start + k, 1), :] = jnp.full(
                    (1, 128), owner, jnp.int32
                )
        return carry

    fetch.wait()
    lax.fori_loop(0, half // 8, gather, 0)


def owner_of(device, columns):
    device = jnp.concatenate([device] * (columns // 128), axis=1)
    return lax.shift_right_logical(device, 1), device & 1


def combine_kernel(where_am_i, keep, got, meta, joined):
    chip, core = where_am_i[0], where_am_i[1]
    half = keep.shape[0]
    owner_chip, owner_core = owner_of(meta[pl.ds(core * half, half), :], keep.shape[1])
    mine = owner_chip == chip
    other = (mine & (owner_core != core)) | (~mine & ((chip == 0) & (core == 1)))
    joined[...] = jnp.where(other, got[...], keep[...])


def halves_kernel(
    where_am_i, joined, before, after, low, high, keep, got, meta, message, pivot_half, top_half
):
    chip, core = where_am_i[0], where_am_i[1]
    half = joined.shape[0]
    owner_chip, owner_core = owner_of(meta[pl.ds(core * half, half), :], joined.shape[1])
    ahead = (owner_chip - chip) & 3
    opposite = jnp.concatenate([low[...], high[...]], axis=0)
    pivot_rows = jnp.where(
        ahead == 0,
        joined[...],
        jnp.where(ahead == 1, after[...], jnp.where(ahead == 3, before[...], opposite)),
    )
    pivot_half[...] = pivot_rows
    top_rows = jnp.where(
        chip == 1, before[...], jnp.where(chip == 3, after[...], opposite)
    )
    top_half[...] = jnp.where(chip == 0, got[...], top_rows)
    message[...] = jnp.where(
        (ahead == 0) & (owner_core != core),
        jnp.where(chip == 0, keep[...], top_rows),
        pivot_rows,
    )


def pair_kernel(own, before, after, three, two):
    size = own.shape[0]
    for k, block in enumerate((own, before, after)):
        three[k * size : (k + 1) * size, :] = block[...]
        if k < 2:
            two[k * size : (k + 1) * size, :] = block[...]


Z_ORDER = (0, -1, 1, -3, -4, -2, 3, 2)


def line_kernel(three, far_before, far_after, line, square):
    for start, block in ((0, three), (24, far_before), (48, far_after)):
        line[start : start + block.shape[0], :] = block[...]
    square[...] = line[:, : square.shape[1]]


def final_kernel(
    where_am_i, places, t_ref, wh_ref, wl_ref, pivot_half, top_half, send, got, meta, out, pivot
):
    chip, core = where_am_i[0], where_am_i[1]
    half = pivot_half.shape[0]
    width = 2 * half
    device = chip * 2 + core
    owner_chip, owner_core = owner_of(
        meta[pl.ds((1 - core) * half, half), :], got.shape[1]
    )
    here = (owner_chip == chip) & (owner_core == core)
    pivot[pl.ds(core * half, half), :] = pivot_half[...]
    pivot[pl.ds((1 - core) * half, half), :] = jnp.where(here, send[...], got[...])
    out[...] = t_ref[...]

    def place(i, carry):
        packed = places[1 + i]
        slot = packed & 255
        target = lax.shift_right_logical(packed, 8) & 1023
        down = jnp.where(device == 0, lax.shift_right_logical(packed, 20), 0)
        index = slot & (half - 1)
        in_half = lax.shift_right_logical(slot, 7) == core
        row = jnp.where(
            device == 0,
            t_ref[pl.ds(down, 1), :],
            jnp.where(in_half, top_half[pl.ds(index, 1), :], got[pl.ds(index, 1), :]),
        )
        out[pl.ds(target, 1), :] = row
        return carry

    lax.fori_loop(0, places[0], place, 0)

    @pl.when(device == 0)
    def _():
        out[0:width, :] = jnp.zeros((width, out.shape[1]), jnp.float32)

    weights = wh_ref[...], wl_ref[...]
    out[...] -= product(weights, split(pivot[...]))


def weights_kernel(where_am_i, line0, line1, line2, line3, wh_ref, wl_ref, stacked):
    width = stacked.shape[0]
    rows = stacked.shape[1] - width
    y, z = where_am_i[2], where_am_i[3]
    size = line0.shape[0] // 8
    for step, line in enumerate((line0, line1, line2, line3)):
        for k, offset in enumerate(Z_ORDER):
            column = ((y - step) & 3) * 8 + ((z + offset) & 7)
            stacked[pl.ds(pl.multiple_of(column * size, size), size), :] = line[
                k * size : (k + 1) * size, :
            ]
    square = stacked[:, rows:]
    row = lax.broadcasted_iota(jnp.int32, (width, width), 0)
    col = lax.broadcasted_iota(jnp.int32, (width, width), 1)
    apart = row ^ col
    inv = jnp.where(row == col, 1.0, 0.0)
    level = 0
    while (1 << level) < width:
        size = 1 << level
        link = (lax.shift_right_logical(apart, level) == 1) & ((col & size) != 0)
        off = jnp.where(link, square, 0.0)
        if level == 0:
            inv = inv - off
        else:
            parts = split(inv)
            inv = inv - product(split(product(parts, split(off))), parts)
        level += 1
    weights = product(split(inv), split(stacked[:, :rows])).T
    high, low = split(weights)
    wh_ref[...] = high
    wl_ref[...] = low

    @pl.when((where_am_i[0] == 0) & (where_am_i[1] == 0))
    def _():
        high, low = split(-inv.T)
        wh_ref[0:width, :] = high
        wl_ref[0:width, :] = low


def device_step(trailing, panel_factors, pivots):
    rows, columns = trailing.shape
    width = pivots.shape[0]
    half = width // 2
    chip, core = lax.axis_index("x"), lax.axis_index("core")
    here = jnp.stack([chip, core, lax.axis_index("y"), lax.axis_index("z")]).astype(jnp.int32)

    panel = panel_factors.T
    before, after = along(panel, "z", 1), along(panel, "z", -1)
    three, two = pl.pallas_call(
        pair_kernel,
        out_shape=(f32(3 * 8, rows), f32(2 * 8, rows)),
        in_specs=[VMEM] * 3,
        out_specs=(VMEM,) * 2,
        compiler_params=PARAMS,
    )(panel, before, after)
    far_before, far_after = along(three, "z", 3), along(two, "z", -3)
    panels, square = pl.pallas_call(
        line_kernel,
        out_shape=(f32(64, rows), f32(64, width)),
        in_specs=[VMEM] * 3,
        out_specs=(VMEM,) * 2,
        compiler_params=PARAMS,
    )(three, far_before, far_after)
    moved = lax.ppermute(square, "core", [(0, 1)])
    square = jnp.where(core == 1, moved, square)
    moved = lax.ppermute(square, "x", [(0, 1)])
    square = jnp.where(chip == 1, moved, square)
    moved = lax.ppermute(square, "x", [(0, 3), (1, 2)])
    square = jnp.where(chip >= 2, moved, square)
    line = jnp.concatenate([panels, square], axis=1)
    lines = [along(line, "y", step) for step in (1, 2, 3)]
    half_weights = jax.ShapeDtypeStruct((rows, width), jnp.bfloat16)
    high, low = pl.pallas_call(
        weights_kernel,
        out_shape=(half_weights, half_weights),
        in_specs=[SMEM] + [VMEM] * 4,
        out_specs=(VMEM, VMEM),
        scratch_shapes=[pltpu.VMEM((width, rows + width), jnp.float32)],
        compiler_params=PARAMS,
    )(here, line, *lines)

    plan = pl.pallas_call(
        plan_kernel,
        out_shape=(
            f32(half, columns),
            f32(half, columns),
            jax.ShapeDtypeStruct((width, 128), jnp.int32),
            jax.ShapeDtypeStruct((512,), jnp.int32),
        ),
        in_specs=[SMEM, SMEM, pl.BlockSpec(memory_space=pltpu.HBM)],
        out_specs=(VMEM, VMEM, VMEM, SMEM),
        scratch_shapes=[
            pltpu.SMEM((rows * 8,), jnp.int32),
            pltpu.SMEM((width,), jnp.int32),
            pltpu.VMEM((rows, columns), jnp.float32),
            pltpu.SemaphoreType.DMA,
        ],
        compiler_params=PARAMS,
    )
    keep, send, meta, places = plan(
        pivots, here, pltpu.with_memory_space_constraint(trailing, pltpu.HBM)
    )
    got = swapped(send, "core", 1)
    combine = pl.pallas_call(
        combine_kernel,
        out_shape=f32(half, columns),
        in_specs=[SMEM, VMEM, VMEM, VMEM],
        out_specs=VMEM,
        compiler_params=PARAMS,
    )
    joined = combine(here, keep, got, meta)
    near_before, near_after = along(joined, "x", 1), along(joined, "x", -1)
    far_low = along(near_before[: half // 2], "x", 1)
    far_high = along(near_after[half // 2 :], "x", -1)
    halves = pl.pallas_call(
        halves_kernel,
        out_shape=(f32(half, columns),) * 3,
        in_specs=[SMEM] + [VMEM] * 8,
        out_specs=(VMEM,) * 3,
        compiler_params=PARAMS,
    )
    message, pivot_half, top_half = halves(
        here, joined, near_before, near_after, far_low, far_high, keep, got, meta
    )
    last = swapped(message, "core", 1)
    return pl.pallas_call(
        final_kernel,
        out_shape=f32(rows, columns),
        in_specs=[SMEM, SMEM] + [VMEM] * 8,
        out_specs=VMEM,
        scratch_shapes=[pltpu.VMEM((width, columns), jnp.float32)],
        compiler_params=PARAMS,
    )(here, places, trailing, high, low, pivot_half, top_half, send, last, meta)


def solution(mesh):
    torus = Mesh(mesh.devices.reshape(4, 2, 4, 8), ("x", "core", "y", "z"))
    return jax.shard_map(
        device_step,
        mesh=torus,
        in_specs=(P(ROW, COL), P(ROW, COL), P()),
        out_specs=P(ROW, COL),
        check_vma=False,
    )
```

```python
import jax
import jax.numpy as jnp
from jax import lax
from jax.experimental import pallas as pl
from jax.experimental.pallas import tpu as pltpu
from jax.sharding import Mesh
from jax.sharding import PartitionSpec as P


ROW = ("x", "core")
COL = ("y", "z")
PARAMS = pltpu.CompilerParams(vmem_limit_bytes=12 * 1024 * 1024)
VMEM = pl.BlockSpec(memory_space=pltpu.VMEM)
SMEM = pl.BlockSpec(memory_space=pltpu.SMEM)


def f32(*shape):
    return jax.ShapeDtypeStruct(shape, jnp.float32)


def along(value, axis, step):
    size = lax.axis_size(axis)
    return lax.ppermute(value, axis, [(i, (i + step) % size) for i in range(size)])


def swapped(value, axis, bit):
    return lax.ppermute(value, axis, [(i, i ^ bit) for i in range(lax.axis_size(axis))])


def split(value):
    high = value.astype(jnp.bfloat16)
    return high, (value - high.astype(jnp.float32)).astype(jnp.bfloat16)


def product(left, right):
    return jnp.dot(
        jnp.concatenate([left[0], left[0], left[1]], axis=1),
        jnp.concatenate([right[0], right[1], right[0]], axis=0),
        preferred_element_type=jnp.float32,
    )


def plan_kernel(piv, where_am_i, t_hbm, keep, send, meta, order, picks, t_ref, arrived):
    fetch = pltpu.make_async_copy(t_hbm, t_ref, arrived)
    fetch.start()
    width = piv.shape[0]
    half = width // 2
    rows = t_ref.shape[0]
    shift = rows.bit_length() - 1
    chip, core = where_am_i[0], where_am_i[1]
    device = chip * 2 + core

    def init(j, carry):
        p = piv[j]
        order[p] = p
        order[j] = j
        return carry

    lax.fori_loop(0, width, init, 0, unroll=16)

    def swap(j, carry):
        p = piv[j]
        a = order[j]
        b = order[p]
        order[j] = b
        order[p] = a
        return carry

    lax.fori_loop(0, width, swap, 0, unroll=16)

    def pick(slot, carry):
        src = order[slot]
        own = lax.shift_right_logical(src, shift) == device
        picks[slot] = jnp.where(own, src, order[src]) & (rows - 1)
        return carry

    lax.fori_loop(0, width, pick, 0, unroll=16)

    def gather(group, carry):
        for base, out in ((core * half, keep), ((1 - core) * half, send)):
            for k in range(8):
                start = pl.multiple_of(group * 8, 8)
                slot = base + start + k
                out[pl.ds(start + k, 1), :] = t_ref[pl.ds(picks[slot], 1), :]
                owner = lax.shift_right_logical(order[slot], shift)
                meta[pl.ds(pl.multiple_of(base, half) + start + k, 1), :] = jnp.full(
                    (1, 128), owner, jnp.int32
                )
        return carry

    fetch.wait()
    lax.fori_loop(0, half // 8, gather, 0)


def list_kernel(order, where_am_i, places):
    width = places.shape[0] // 2
    device = where_am_i[0] * 2 + where_am_i[1]
    rows = order.shape[0] // 8
    shift = rows.bit_length() - 1

    def visit(slot, count):
        src = order[slot]
        places[1 + count] = slot | ((src & (rows - 1)) << 8) | (order[src] << 20)
        own = lax.shift_right_logical(src, shift) == device
        return count + jnp.where(own & (src >= width), 1, 0)

    places[0] = lax.fori_loop(0, width, visit, 0, unroll=8)


def owner_of(device, columns):
    device = jnp.concatenate([device] * (columns // 128), axis=1)
    return lax.shift_right_logical(device, 1), device & 1


def combine_kernel(where_am_i, keep, got, meta, joined):
    chip, core = where_am_i[0], where_am_i[1]
    half = keep.shape[0]
    owner_chip, owner_core = owner_of(meta[pl.ds(core * half, half), :], keep.shape[1])
    mine = owner_chip == chip
    other = (mine & (owner_core != core)) | (~mine & ((chip == 0) & (core == 1)))
    joined[...] = jnp.where(other, got[...], keep[...])


def halves_kernel(
    where_am_i, joined, before, after, low, high, keep, got, meta, message, pivot_half, top_half
):
    chip, core = where_am_i[0], where_am_i[1]
    half = joined.shape[0]
    owner_chip, owner_core = owner_of(meta[pl.ds(core * half, half), :], joined.shape[1])
    ahead = (owner_chip - chip) & 3
    opposite = jnp.concatenate([low[...], high[...]], axis=0)
    pivot_rows = jnp.where(
        ahead == 0,
        joined[...],
        jnp.where(ahead == 1, after[...], jnp.where(ahead == 3, before[...], opposite)),
    )
    pivot_half[...] = pivot_rows
    top_rows = jnp.where(
        chip == 1, before[...], jnp.where(chip == 3, after[...], opposite)
    )
    top_half[...] = jnp.where(chip == 0, got[...], top_rows)
    message[...] = jnp.where(
        (ahead == 0) & (owner_core != core),
        jnp.where(chip == 0, keep[...], top_rows),
        pivot_rows,
    )


def pair_kernel(own, before, after, three, two):
    size = own.shape[0]
    for k, block in enumerate((own, before, after)):
        three[k * size : (k + 1) * size, :] = block[...]
        if k < 2:
            two[k * size : (k + 1) * size, :] = block[...]


Z_ORDER = (0, -1, 1, -3, -4, -2, 3, 2)


def line_kernel(three, far_before, far_after, line, square):
    for start, block in ((0, three), (24, far_before), (48, far_after)):
        line[start : start + block.shape[0], :] = block[...]
    square[...] = line[:, : square.shape[1]]


def final_kernel(
    where_am_i, places, t_ref, w_ref, pivot_half, top_half, send, got, meta, result, pivot, out, done
):
    chip, core = where_am_i[0], where_am_i[1]
    rows = t_ref.shape[0]
    half = pivot_half.shape[0]
    width = 2 * half
    device = chip * 2 + core
    owner_chip, owner_core = owner_of(
        meta[pl.ds((1 - core) * half, half), :], got.shape[1]
    )
    here = (owner_chip == chip) & (owner_core == core)
    pivot[pl.ds(core * half, half), :] = pivot_half[...]
    pivot[pl.ds((1 - core) * half, half), :] = jnp.where(here, send[...], got[...])
    out[...] = t_ref[...]

    def place(i, carry):
        packed = places[1 + i]
        slot = packed & 255
        target = lax.shift_right_logical(packed, 8) & 1023
        down = jnp.where(device == 0, lax.shift_right_logical(packed, 20), 0)
        index = slot & (half - 1)
        in_half = lax.shift_right_logical(slot, 7) == core
        row = jnp.where(
            device == 0,
            t_ref[pl.ds(down, 1), :],
            jnp.where(in_half, top_half[pl.ds(index, 1), :], got[pl.ds(index, 1), :]),
        )
        out[pl.ds(target, 1), :] = row
        return carry

    lax.fori_loop(0, places[0], place, 0)

    @pl.when(device == 0)
    def _():
        out[0:width, :] = jnp.zeros((width, out.shape[1]), jnp.float32)

    high, low = split(pivot[...])
    rows_in = jnp.concatenate([high, low, high], axis=0)
    copies = []
    for k in range(4):
        band = pl.ds(k * rows // 4, rows // 4)
        out[band, :] -= jnp.dot(
            w_ref[band, :], rows_in, preferred_element_type=jnp.float32
        )
        copies.append(pltpu.make_async_copy(out.at[band, :], result.at[band, :], done.at[k]))
        copies[-1].start()
    for copy in copies:
        copy.wait()


def weights_kernel(where_am_i, line0, line1, line2, line3, w_ref, stacked):
    width = stacked.shape[0]
    rows = stacked.shape[1] - width
    y, z = where_am_i[2], where_am_i[3]
    size = line0.shape[0] // 8
    for step, line in enumerate((line0, line1, line2, line3)):
        for k, offset in enumerate(Z_ORDER):
            column = ((y - step) & 3) * 8 + ((z + offset) & 7)
            stacked[pl.ds(pl.multiple_of(column * size, size), size), :] = line[
                k * size : (k + 1) * size, :
            ]
    block = width // 2
    row = lax.broadcasted_iota(jnp.int32, (block, block), 0)
    col = lax.broadcasted_iota(jnp.int32, (block, block), 1)
    apart = row ^ col

    def inverse(square):
        inv = jnp.where(row == col, 1.0, 0.0)
        level = 0
        while (1 << level) < block:
            wide = (1 << level + 1) < block
            far = lax.shift_right_logical(apart, level)
            link = (far > 0) & (far < (4 if wide else 2)) & (row < col)
            off = split(jnp.where(link, square, 0.0))
            if level == 0:
                step = jnp.where(link, square, 0.0)
                parts = split(step)
                inv = inv - step
            else:
                parts = split(product(split(inv), off))
                inv = inv - product(parts, split(inv))
            if wide:
                twice = product(parts, parts)
                inv = inv + product(split(twice), split(inv))
            level += 2
        return inv

    first = inverse(stacked[0:block, rows : rows + block])
    second = inverse(stacked[block:, rows + block :])
    corner = product(
        split(product(split(first), split(stacked[0:block, rows + block :]))), split(second)
    )
    inv = jnp.concatenate(
        [
            jnp.concatenate([first, -corner], axis=1),
            jnp.concatenate([jnp.zeros_like(corner), second], axis=1),
        ],
        axis=0,
    )
    factors = stacked[:, :rows].T
    top = (where_am_i[0] == 0) & (where_am_i[1] == 0)
    here = lax.broadcasted_iota(jnp.int32, (width, width), 0)
    there = lax.broadcasted_iota(jnp.int32, (width, width), 1)
    minus_one = jnp.where(here == there, -1.0, 0.0)
    factors = jnp.concatenate(
        [jnp.where(top, minus_one, factors[0:width, :]), factors[width:, :]], axis=0
    )
    a, b = split(factors), split(inv)
    weights = lax.dot_general(
        jnp.concatenate([a[0], a[0], a[1]], axis=1),
        jnp.concatenate([b[0], b[1], b[0]], axis=1),
        (((1,), (1,)), ((), ())),
        preferred_element_type=jnp.float32,
    )
    high, low = split(weights)
    w_ref[...] = jnp.concatenate([high, high, low], axis=1)


def device_step(trailing, panel_factors, pivots):
    rows, columns = trailing.shape
    width = pivots.shape[0]
    half = width // 2
    chip, core = lax.axis_index("x"), lax.axis_index("core")
    here = jnp.stack([chip, core, lax.axis_index("y"), lax.axis_index("z")]).astype(jnp.int32)

    panel = panel_factors.T
    before, after = along(panel, "z", 1), along(panel, "z", -1)
    three, two = pl.pallas_call(
        pair_kernel,
        out_shape=(f32(3 * 8, rows), f32(2 * 8, rows)),
        in_specs=[VMEM] * 3,
        out_specs=(VMEM,) * 2,
        compiler_params=PARAMS,
    )(panel, before, after)
    far_before, far_after = along(three, "z", 3), along(two, "z", -3)
    panels, square = pl.pallas_call(
        line_kernel,
        out_shape=(f32(64, rows), f32(64, width)),
        in_specs=[VMEM] * 3,
        out_specs=(VMEM,) * 2,
        compiler_params=PARAMS,
    )(three, far_before, far_after)
    moved = swapped(square, "core", 1)
    square = jnp.where(core == 1, moved, square)
    ways = [(i, (i + (2 if i % 2 == 0 else 6)) % 8) for i in range(8)]
    near = lax.ppermute(square, ROW, ways)
    far = along(square, "x", 2)
    square = jnp.where(chip == 0, square, jnp.where(chip == 2, far, near))
    moved = swapped(square, "core", 1)
    square = jnp.where((chip & 1 == 1) & (core == (chip >> 1 ^ 1)), moved, square)
    line = jnp.concatenate([panels, square], axis=1)
    lines = [along(line, "y", step) for step in (1, 2, 3)]
    weights = pl.pallas_call(
        weights_kernel,
        out_shape=jax.ShapeDtypeStruct((rows, 3 * width), jnp.bfloat16),
        in_specs=[SMEM] + [VMEM] * 4,
        out_specs=VMEM,
        scratch_shapes=[pltpu.VMEM((width, rows + width), jnp.float32)],
        compiler_params=PARAMS,
    )(here, line, *lines)

    plan = pl.pallas_call(
        plan_kernel,
        out_shape=(
            f32(half, columns),
            f32(half, columns),
            jax.ShapeDtypeStruct((width, 128), jnp.int32),
            jax.ShapeDtypeStruct((rows * 8,), jnp.int32),
        ),
        in_specs=[SMEM, SMEM, pl.BlockSpec(memory_space=pltpu.HBM)],
        out_specs=(VMEM, VMEM, VMEM, SMEM),
        scratch_shapes=[
            pltpu.SMEM((width,), jnp.int32),
            pltpu.VMEM((rows, columns), jnp.float32),
            pltpu.SemaphoreType.DMA,
        ],
        compiler_params=PARAMS,
    )
    keep, send, meta, order = plan(
        pivots, here, pltpu.with_memory_space_constraint(trailing, pltpu.HBM)
    )
    got = swapped(send, "core", 1)
    combine = pl.pallas_call(
        combine_kernel,
        out_shape=f32(half, columns),
        in_specs=[SMEM, VMEM, VMEM, VMEM],
        out_specs=VMEM,
        compiler_params=PARAMS,
    )
    joined = combine(here, keep, got, meta)
    near_before, near_after = along(joined, "x", 1), along(joined, "x", -1)
    far_low = along(near_before[: half // 2], "x", 1)
    far_high = along(near_after[half // 2 :], "x", -1)
    halves = pl.pallas_call(
        halves_kernel,
        out_shape=(f32(half, columns),) * 3,
        in_specs=[SMEM] + [VMEM] * 8,
        out_specs=(VMEM,) * 3,
        compiler_params=PARAMS,
    )
    message, pivot_half, top_half = halves(
        here, joined, near_before, near_after, far_low, far_high, keep, got, meta
    )
    listing = pl.pallas_call(
        list_kernel,
        out_shape=jax.ShapeDtypeStruct((2 * width,), jnp.int32),
        in_specs=[SMEM, SMEM],
        out_specs=SMEM,
        compiler_params=PARAMS,
    )
    places = listing(order, here)
    last = swapped(message, "core", 1)
    return pl.pallas_call(
        final_kernel,
        out_shape=f32(rows, columns),
        in_specs=[SMEM, SMEM] + [VMEM] * 7,
        out_specs=pl.BlockSpec(memory_space=pltpu.HBM),
        scratch_shapes=[
            pltpu.VMEM((width, columns), jnp.float32),
            pltpu.VMEM((rows, columns), jnp.float32),
            pltpu.SemaphoreType.DMA((4,)),
        ],
        compiler_params=PARAMS,
    )(here, places, trailing, weights, pivot_half, top_half, send, last, meta)


def solution(mesh):
    torus = Mesh(mesh.devices.reshape(4, 2, 4, 8), ("x", "core", "y", "z"))
    return jax.shard_map(
        device_step,
        mesh=torus,
        in_specs=(P(ROW, COL), P(ROW, COL), P()),
        out_specs=P(ROW, COL),
        check_vma=False,
    )
```

```python
import jax
import jax.numpy as jnp
from jax import lax
from jax.experimental import pallas as pl
from jax.experimental.pallas import tpu as pltpu
from jax.sharding import Mesh
from jax.sharding import PartitionSpec as P


ROW = ("x", "core")
COL = ("y", "z")
PARAMS = pltpu.CompilerParams(vmem_limit_bytes=12 * 1024 * 1024)
VMEM = pl.BlockSpec(memory_space=pltpu.VMEM)
SMEM = pl.BlockSpec(memory_space=pltpu.SMEM)


def f32(*shape):
    return jax.ShapeDtypeStruct(shape, jnp.float32)


def along(value, axis, step):
    size = lax.axis_size(axis)
    return lax.ppermute(value, axis, [(i, (i + step) % size) for i in range(size)])


def swapped(value, axis, bit):
    return lax.ppermute(value, axis, [(i, i ^ bit) for i in range(lax.axis_size(axis))])


def split(value):
    high = value.astype(jnp.bfloat16)
    return high, (value - high.astype(jnp.float32)).astype(jnp.bfloat16)


def product(left, right):
    return jnp.dot(
        jnp.concatenate([left[0], left[0], left[1]], axis=1),
        jnp.concatenate([right[0], right[1], right[0]], axis=0),
        preferred_element_type=jnp.float32,
    )


def plan_kernel(piv, where_am_i, t_hbm, keep, send, meta, order, picks, t_ref, arrived):
    fetch = pltpu.make_async_copy(t_hbm, t_ref, arrived)
    fetch.start()
    width = piv.shape[0]
    half = width // 2
    rows = t_ref.shape[0]
    shift = rows.bit_length() - 1
    chip, core = where_am_i[0], where_am_i[1]
    device = chip * 2 + core

    def init(j, carry):
        p = piv[j]
        order[p] = p
        order[j] = j
        return carry

    lax.fori_loop(0, width, init, 0, unroll=16)

    def swap(j, carry):
        p = piv[j]
        a = order[j]
        b = order[p]
        order[j] = b
        order[p] = a
        return carry

    lax.fori_loop(0, width, swap, 0, unroll=16)

    def pick(slot, carry):
        src = order[slot]
        own = lax.shift_right_logical(src, shift) == device
        picks[slot] = jnp.where(own, src, order[src]) & (rows - 1)
        return carry

    lax.fori_loop(0, width, pick, 0, unroll=16)

    def gather(group, carry):
        for base, out in ((core * half, keep), ((1 - core) * half, send)):
            for k in range(8):
                start = pl.multiple_of(group * 8, 8)
                slot = base + start + k
                out[pl.ds(start + k, 1), :] = t_ref[pl.ds(picks[slot], 1), :]
                owner = lax.shift_right_logical(order[slot], shift)
                meta[pl.ds(pl.multiple_of(base, half) + start + k, 1), :] = jnp.full(
                    (1, 128), owner, jnp.int32
                )
        return carry

    fetch.wait()
    lax.fori_loop(0, half // 8, gather, 0)


def list_kernel(order, where_am_i, places):
    width = places.shape[0] // 2
    device = where_am_i[0] * 2 + where_am_i[1]
    rows = order.shape[0] // 8
    shift = rows.bit_length() - 1

    def visit(slot, count):
        src = order[slot]
        places[1 + count] = slot | ((src & (rows - 1)) << 8) | (order[src] << 20)
        own = lax.shift_right_logical(src, shift) == device
        return count + jnp.where(own & (src >= width), 1, 0)

    places[0] = lax.fori_loop(0, width, visit, 0, unroll=8)


def owner_of(device, columns):
    device = jnp.concatenate([device] * (columns // 128), axis=1)
    return lax.shift_right_logical(device, 1), device & 1


def combine_kernel(where_am_i, keep, got, meta, joined):
    chip, core = where_am_i[0], where_am_i[1]
    half = keep.shape[0]
    owner_chip, owner_core = owner_of(meta[pl.ds(core * half, half), :], keep.shape[1])
    mine = owner_chip == chip
    other = (mine & (owner_core != core)) | (~mine & ((chip == 0) & (core == 1)))
    joined[...] = jnp.where(other, got[...], keep[...])


def halves_kernel(
    where_am_i, joined, before, after, low, high, keep, got, meta, message, pivot_half, top_half
):
    chip, core = where_am_i[0], where_am_i[1]
    half = joined.shape[0]
    owner_chip, owner_core = owner_of(meta[pl.ds(core * half, half), :], joined.shape[1])
    ahead = (owner_chip - chip) & 3
    opposite = jnp.concatenate([low[...], high[...]], axis=0)
    pivot_rows = jnp.where(
        ahead == 0,
        joined[...],
        jnp.where(ahead == 1, after[...], jnp.where(ahead == 3, before[...], opposite)),
    )
    pivot_half[...] = pivot_rows
    top_rows = jnp.where(
        chip == 1, before[...], jnp.where(chip == 3, after[...], opposite)
    )
    top_half[...] = jnp.where(chip == 0, got[...], top_rows)
    message[...] = jnp.where(
        (ahead == 0) & (owner_core != core),
        jnp.where(chip == 0, keep[...], top_rows),
        pivot_rows,
    )


def pair_kernel(own, before, after, three, two):
    size = own.shape[0]
    for k, block in enumerate((own, before, after)):
        three[k * size : (k + 1) * size, :] = block[...]
        if k < 2:
            two[k * size : (k + 1) * size, :] = block[...]


Z_ORDER = (0, -1, 1, -3, -4, -2, 3, 2)


def line_kernel(three, far_before, far_after, line, square):
    for start, block in ((0, three), (24, far_before), (48, far_after)):
        line[start : start + block.shape[0], :] = block[...]
    square[...] = line[:, : square.shape[1]]


def final_kernel(
    where_am_i, places, t_ref, w_ref, pivot_half, top_half, send, got, meta, result, pivot, out, done
):
    chip, core = where_am_i[0], where_am_i[1]
    rows = t_ref.shape[0]
    half = pivot_half.shape[0]
    width = 2 * half
    device = chip * 2 + core
    owner_chip, owner_core = owner_of(
        meta[pl.ds((1 - core) * half, half), :], got.shape[1]
    )
    here = (owner_chip == chip) & (owner_core == core)
    pivot[pl.ds(core * half, half), :] = pivot_half[...]
    pivot[pl.ds((1 - core) * half, half), :] = jnp.where(here, send[...], got[...])
    out[...] = t_ref[...]

    def place(i, carry):
        packed = places[1 + i]
        slot = packed & 255
        target = lax.shift_right_logical(packed, 8) & 1023
        down = jnp.where(device == 0, lax.shift_right_logical(packed, 20), 0)
        index = slot & (half - 1)
        in_half = lax.shift_right_logical(slot, 7) == core
        row = jnp.where(
            device == 0,
            t_ref[pl.ds(down, 1), :],
            jnp.where(in_half, top_half[pl.ds(index, 1), :], got[pl.ds(index, 1), :]),
        )
        out[pl.ds(target, 1), :] = row
        return carry

    lax.fori_loop(0, places[0], place, 0)

    @pl.when(device == 0)
    def _():
        out[0:width, :] = jnp.zeros((width, out.shape[1]), jnp.float32)

    high, low = split(pivot[...])
    rows_in = jnp.concatenate([high, low, high], axis=0)
    copies = []
    for k in range(4):
        band = pl.ds(k * rows // 4, rows // 4)
        out[band, :] -= jnp.dot(
            w_ref[band, :], rows_in, preferred_element_type=jnp.float32
        )
        copies.append(pltpu.make_async_copy(out.at[band, :], result.at[band, :], done.at[k]))
        copies[-1].start()
    for copy in copies:
        copy.wait()


def weights_kernel(where_am_i, line0, line1, line2, line3, w_ref, stacked):
    width = stacked.shape[0]
    rows = stacked.shape[1] - width
    y, z = where_am_i[2], where_am_i[3]
    size = line0.shape[0] // 8
    for step, line in enumerate((line0, line1, line2, line3)):
        for k, offset in enumerate(Z_ORDER):
            column = ((y - step) & 3) * 8 + ((z + offset) & 7)
            stacked[pl.ds(pl.multiple_of(column * size, size), size), :] = line[
                k * size : (k + 1) * size, :
            ]
    block = width // 2
    row = lax.broadcasted_iota(jnp.int32, (block, block), 0)
    col = lax.broadcasted_iota(jnp.int32, (block, block), 1)
    apart = row ^ col

    def inverse(square):
        inv = jnp.where(row == col, 1.0, 0.0)
        level = 0
        while (1 << level) < block:
            wide = (1 << level + 1) < block
            far = lax.shift_right_logical(apart, level)
            link = (far > 0) & (far < (4 if wide else 2)) & (row < col)
            off = split(jnp.where(link, square, 0.0))
            if level == 0:
                step = jnp.where(link, square, 0.0)
                parts = split(step)
                inv = inv - step
            else:
                parts = split(product(split(inv), off))
                inv = inv - product(parts, split(inv))
            if wide:
                twice = product(parts, parts)
                inv = inv + product(split(twice), split(inv))
            level += 2
        return inv

    first = inverse(stacked[0:block, rows : rows + block])
    second = inverse(stacked[block:, rows + block :])
    corner = product(
        split(product(split(first), split(stacked[0:block, rows + block :]))), split(second)
    )
    inv = jnp.concatenate(
        [
            jnp.concatenate([first, -corner], axis=1),
            jnp.concatenate([jnp.zeros_like(corner), second], axis=1),
        ],
        axis=0,
    )
    factors = stacked[:, :rows].T
    top = (where_am_i[0] == 0) & (where_am_i[1] == 0)
    here = lax.broadcasted_iota(jnp.int32, (width, width), 0)
    there = lax.broadcasted_iota(jnp.int32, (width, width), 1)
    minus_one = jnp.where(here == there, -1.0, 0.0)
    factors = jnp.concatenate(
        [jnp.where(top, minus_one, factors[0:width, :]), factors[width:, :]], axis=0
    )
    a, b = split(factors), split(inv)
    weights = lax.dot_general(
        jnp.concatenate([a[0], a[0], a[1]], axis=1),
        jnp.concatenate([b[0], b[1], b[0]], axis=1),
        (((1,), (1,)), ((), ())),
        preferred_element_type=jnp.float32,
    )
    high, low = split(weights)
    w_ref[...] = jnp.concatenate([high, high, low], axis=1)


def device_step(trailing, panel_factors, pivots):
    rows, columns = trailing.shape
    width = pivots.shape[0]
    half = width // 2
    chip, core = lax.axis_index("x"), lax.axis_index("core")
    here = jnp.stack([chip, core, lax.axis_index("y"), lax.axis_index("z")]).astype(jnp.int32)

    panel = panel_factors.T
    before, after = along(panel, "z", 1), along(panel, "z", -1)
    three, two = pl.pallas_call(
        pair_kernel,
        out_shape=(f32(3 * 8, rows), f32(2 * 8, rows)),
        in_specs=[VMEM] * 3,
        out_specs=(VMEM,) * 2,
        compiler_params=PARAMS,
    )(panel, before, after)
    far_before, far_after = along(three, "z", 3), along(two, "z", -3)
    panels, square = pl.pallas_call(
        line_kernel,
        out_shape=(f32(64, rows), f32(64, width)),
        in_specs=[VMEM] * 3,
        out_specs=(VMEM,) * 2,
        compiler_params=PARAMS,
    )(three, far_before, far_after)
    moved = swapped(square, "core", 1)
    square = jnp.where(core == 1, moved, square)
    ways = [(i, (i + (2 if i % 2 == 0 else 6)) % 8) for i in range(8)]
    near = lax.ppermute(square, ROW, ways)
    far = along(square, "x", 2)
    moved = swapped(near, "core", 1)
    near = jnp.where(core == chip >> 1, near, moved)
    square = jnp.where(chip == 0, square, jnp.where(chip == 2, far, near))
    line = jnp.concatenate([panels, square], axis=1)
    second = along(line, "y", 2)
    lines = [along(line, "y", 1), second, along(line, "y", 3)]
    weights = pl.pallas_call(
        weights_kernel,
        out_shape=jax.ShapeDtypeStruct((rows, 3 * width), jnp.bfloat16),
        in_specs=[SMEM] + [VMEM] * 4,
        out_specs=VMEM,
        scratch_shapes=[pltpu.VMEM((width, rows + width), jnp.float32)],
        compiler_params=PARAMS,
    )(here, line, *lines)

    plan = pl.pallas_call(
        plan_kernel,
        out_shape=(
            f32(half, columns),
            f32(half, columns),
            jax.ShapeDtypeStruct((width, 128), jnp.int32),
            jax.ShapeDtypeStruct((rows * 8,), jnp.int32),
        ),
        in_specs=[SMEM, SMEM, pl.BlockSpec(memory_space=pltpu.HBM)],
        out_specs=(VMEM, VMEM, VMEM, SMEM),
        scratch_shapes=[
            pltpu.SMEM((width,), jnp.int32),
            pltpu.VMEM((rows, columns), jnp.float32),
            pltpu.SemaphoreType.DMA,
        ],
        compiler_params=PARAMS,
    )
    targets = jnp.minimum(pivots, rows * 8 - 1)
    keep, send, meta, order = plan(
        targets, here, pltpu.with_memory_space_constraint(trailing, pltpu.HBM)
    )
    got = swapped(send, "core", 1)
    combine = pl.pallas_call(
        combine_kernel,
        out_shape=f32(half, columns),
        in_specs=[SMEM, VMEM, VMEM, VMEM],
        out_specs=VMEM,
        compiler_params=PARAMS,
    )
    joined = combine(here, keep, got, meta)
    near_before, near_after = along(joined, "x", 1), along(joined, "x", -1)
    far_high = along(near_after[half // 2 :], "x", -1)
    far_low = along(near_before[: half // 2], "x", 1)
    halves = pl.pallas_call(
        halves_kernel,
        out_shape=(f32(half, columns),) * 3,
        in_specs=[SMEM] + [VMEM] * 8,
        out_specs=(VMEM,) * 3,
        compiler_params=PARAMS,
    )
    message, pivot_half, top_half = halves(
        here, joined, near_before, near_after, far_low, far_high, keep, got, meta
    )
    listing = pl.pallas_call(
        list_kernel,
        out_shape=jax.ShapeDtypeStruct((2 * width,), jnp.int32),
        in_specs=[SMEM, SMEM],
        out_specs=SMEM,
        compiler_params=PARAMS,
    )
    places = listing(order, here)
    last = swapped(message, "core", 1)
    return pl.pallas_call(
        final_kernel,
        out_shape=f32(rows, columns),
        in_specs=[SMEM, SMEM] + [VMEM] * 7,
        out_specs=pl.BlockSpec(memory_space=pltpu.HBM),
        scratch_shapes=[
            pltpu.VMEM((width, columns), jnp.float32),
            pltpu.VMEM((rows, columns), jnp.float32),
            pltpu.SemaphoreType.DMA((4,)),
        ],
        compiler_params=PARAMS,
    )(here, places, trailing, weights, pivot_half, top_half, send, last, meta)


def solution(mesh):
    torus = Mesh(mesh.devices.reshape(4, 2, 4, 8), ("x", "core", "y", "z"))
    return jax.shard_map(
        device_step,
        mesh=torus,
        in_specs=(P(ROW, COL), P(ROW, COL), P()),
        out_specs=P(ROW, COL),
        check_vma=False,
    )
```
